32 devices in a mesh: dom: 32 (over z, y, x, core).
Axes of the slice: x: 2, y: 2, z: 4, core: 2. Of those that a mesh axis runs over, the one named last changes fastest.
Arguments:
- entities: float32 [32768, 200], P('dom'), may hold values from -3 to 3
- entity_state: float32 [32768], P('dom'), may hold values from 1e-05 to 0.1
- relations: float32 [1345, 200], replicated, may hold values from -3 to 3
- relation_state: float32 [1345], replicated, may hold values from 1 to 100
- edges: int32 [2, 3, 16384], P(None, None, 'dom'), may hold values from 0 to 1344, as said below
- negatives: int32 [2, 128, 1000], P(None, 'dom'), may hold values from 0 to 1023
- counts: int32 [2, 32], P(None, 'dom'), may hold values from 1 to 512, as said below
Outputs:
- entities_after: float32 [32768, 200], P('dom')
- entity_state_after: float32 [32768], P('dom')
- relations_after: float32 [1345, 200], replicated
- relation_state_after: float32 [1345], replicated
The draws below stay inside these ranges and needn't reach their ends.
Inputs may be any that keep to these rules, and one draw needn't show every extreme that they name: `edges`: rows 0 and 2 are local entity ids below 1024; row 1 holds relation ids below 1345. `negatives`: local ids in the partner's partition. `counts`: in every round some bucket is full.
All inputs are finite; a program needn't handle non-finite values.
Results may differ from the reference program's by a relative error of at most 0.0003.
Values sent between devices are 32-bit elements; how exact they have to be, the bound alone decides.
A program may use at most 64 MiB of HBM per device.

```python
import math
import jax
import jax.numpy as jnp
from jax import lax

ENT_DEV = 1024
DIM = 200
REL = 1345
NEG = 1000
BLOCK = 128
BLOCKS = 4
ROUNDS = 2
EDGES_DEV = 512
PARTITIONS = 32
ENTITIES = 32768
TOTAL_EDGES = 16384
ALL_BLOCKS = 128


def draw_edges(key, part):
    keys = jax.random.split(jax.random.fold_in(key, 11), 4)
    source = jax.random.randint(keys[0], (ROUNDS, 1, TOTAL_EDGES), 0, ENT_DEV, dtype=jnp.int32)
    target = jax.random.randint(keys[1], (ROUNDS, 1, TOTAL_EDGES), 0, ENT_DEV, dtype=jnp.int32)
    first = jax.random.randint(keys[2], (ROUNDS, 1, TOTAL_EDGES), 0, REL, dtype=jnp.int32)
    second = jax.random.randint(keys[3], (ROUNDS, 1, TOTAL_EDGES), 0, REL, dtype=jnp.int32)
    relation = first * second // REL
    return jnp.concatenate([source, relation, target], axis=1).astype(jnp.int32)


def draw_counts(key, part):
    keys = jax.random.split(jax.random.fold_in(key, 23), 3)
    first = jax.random.randint(keys[0], (ROUNDS, PARTITIONS), 0, EDGES_DEV, dtype=jnp.int32)
    second = jax.random.randint(keys[1], (ROUNDS, PARTITIONS), 0, EDGES_DEV, dtype=jnp.int32)
    filled = 1 + first * second // EDGES_DEV
    fullest = jax.random.randint(keys[2], (ROUNDS, 1), 0, PARTITIONS, dtype=jnp.int32)
    places = jnp.arange(PARTITIONS, dtype=jnp.int32)[None, :]
    return jnp.where(places == fullest, EDGES_DEV, filled).astype(jnp.int32)


def set_ends(values, rng, smallest, high):
    extent = values.shape
    place = [jax.random.randint(jax.random.fold_in(rng, axis), (), 0, extent[axis]) for axis in range(len(extent))]
    values = values.at[tuple(place)].set(smallest)
    longest = extent.index(max(extent))
    place[longest] = (place[longest] + 1) % extent[longest]
    return values.at[tuple(place)].set(high)


def shard_levels(key, extent, cuts, smallest, high):
    def one(dim, parts):
        heights = jax.random.uniform(jax.random.fold_in(jax.random.fold_in(key, 6), dim), (parts,), jnp.float32, smallest / len(cuts), high / len(cuts))
        return jnp.repeat(jnp.exp(heights), extent[dim] // parts).reshape((-1,) + (1,) * (len(extent) - dim - 1))

    loudness = one(*cuts[0])
    for cut in cuts[1:]:
        loudness = loudness * one(*cut)
    return loudness


def scatter_about(stream_key, dims, scale, bound, shards=(), kind=jnp.bfloat16):
    drawn = scale * jax.random.normal(stream_key, dims, jnp.float32)
    if shards:
        drawn = drawn * shard_levels(stream_key, dims, shards, -0.22, 0.18)
    return jnp.clip(drawn, -bound, bound).astype(kind)


def setup_inputs(seed: int = 0) -> dict:
    seeds = jax.random.split(jax.random.key(seed), 8)
    return {
        "entities": scatter_about(seeds[0], (ENTITIES, DIM), 0.5, 3.0, ((0, 32),), jnp.float32),
        "entity_state": jnp.clip(jnp.exp(math.log(0.1) - 9.2103404 * jax.random.uniform(seeds[1], (ENTITIES,), jnp.float32) ** shard_levels(seeds[1], (ENTITIES,), ((0, 32),), -0.2, 0.2)), 9.999999747378752e-06, 0.1),
        "relations": scatter_about(seeds[2], (REL, DIM), 0.5, 3.0, (), jnp.float32),
        "relation_state": jnp.clip(jnp.exp(jax.random.uniform(seeds[3], (REL,), jnp.float32, math.log(1.0), math.log(100.0))), 1.0, 100.0),
        "edges": draw_edges(jax.random.fold_in(seeds[7], 71), 0),
        "negatives": set_ends(jax.random.randint(seeds[5], (ROUNDS, ALL_BLOCKS, NEG), 0, ENT_DEV), jax.random.fold_in(seeds[5], 1), 0, ENT_DEV - 1).astype(jnp.int32),
        "counts": draw_counts(jax.random.fold_in(seeds[7], 71), 0),
    }


RATE = 0.2
HIGH = lax.Precision.HIGHEST

def block_terms(carry, table, relations, source, relation, target, negative_ids, live):
    grad_table, grad_relation = carry
    half = table.shape[1] // 2
    src_rows = table[source]
    tgt_rows = table[target]
    neg_rows = table[negative_ids]
    rel_rows = relations[relation]
    src_real, src_imag = (src_rows[:, :half], src_rows[:, half:])
    rel_real, rel_imag = (rel_rows[:, :half], rel_rows[:, half:])
    product = jnp.concatenate([src_real * rel_real - src_imag * rel_imag, src_real * rel_imag + src_imag * rel_real], axis=1)
    positive = lax.optimization_barrier(jnp.sum(product * tgt_rows, axis=1))
    negative = lax.dot_general(product, neg_rows, (((1,), (1,)), ((), ())), precision=HIGH, preferred_element_type=jnp.float32)
    pos_weight = -jax.nn.sigmoid(-positive) * live
    neg_weight = jax.nn.sigmoid(negative) * (live[:, None] / negative.shape[1])
    upstream = pos_weight[:, None] * tgt_rows + jnp.dot(neg_weight, neg_rows, precision=HIGH, preferred_element_type=jnp.float32)
    target_grad = pos_weight[:, None] * product
    negative_grad = lax.dot_general(neg_weight, product, (((0,), (0,)), ((), ())), precision=HIGH, preferred_element_type=jnp.float32)
    up_real, up_imag = (upstream[:, :half], upstream[:, half:])
    source_grad = jnp.concatenate([up_real * rel_real + up_imag * rel_imag, up_imag * rel_real - up_real * rel_imag], axis=1)
    relation_grad = jnp.concatenate([up_real * src_real + up_imag * src_imag, up_imag * src_real - up_real * src_imag], axis=1)
    grad_table = grad_table.at[source].add(source_grad).at[target].add(target_grad).at[negative_ids].add(negative_grad)
    grad_relation = grad_relation.at[relation].add(relation_grad)
    return (grad_table, grad_relation)

def bucket_pass(carry, table, relations, edge_pair, negative_pair, count_pair, source_shift, target_shift, block, first, last):
    block_pair = (count_pair + block - 1) // block

    def visit(index, inner):
        which = (index >= block_pair[0]).astype(jnp.int32)
        number = (index - which * block_pair[0]).astype(jnp.int32)
        edge_list = lax.dynamic_index_in_dim(edge_pair, which, 0, keepdims=False)
        start = (number * block).astype(jnp.int32)
        window = lax.dynamic_slice_in_dim(edge_list, start, block, 1)
        negative_list = lax.dynamic_index_in_dim(negative_pair, which, 0, keepdims=False)
        negative_ids = lax.dynamic_index_in_dim(negative_list, number, 0, keepdims=False) + target_shift[which]
        live = (start + jnp.arange(block, dtype=jnp.int32) < count_pair[which]).astype(jnp.float32)
        return block_terms(inner, table, relations, window[0] + source_shift[which], window[1], window[2] + target_shift[which], negative_ids, live)
    return lax.fori_loop(first, last, visit, carry)

def adagrad(param, state, grad):
    new_state = state + lax.optimization_barrier(jnp.mean(grad * grad, axis=1))
    return (param - RATE * grad / jnp.sqrt(new_state)[:, None], new_state)

def round_pass(entities, entity_state, relations, edge_round, negative_round, count_round, span):
    source_shift = jnp.array([0, ENT_DEV], dtype=jnp.int32)
    target_shift = jnp.array([ENT_DEV, 0], dtype=jnp.int32)

    def visit_pair(pair, carry):
        new_entities, new_state, grad_relation = carry
        pair = pair.astype(jnp.int32)
        lower = (pair // span * (2 * span) + pair % span).astype(jnp.int32)
        upper = (lower + span).astype(jnp.int32)
        low_rows = lax.dynamic_slice_in_dim(entities, (lower * ENT_DEV).astype(jnp.int32), ENT_DEV, 0)
        high_rows = lax.dynamic_slice_in_dim(entities, (upper * ENT_DEV).astype(jnp.int32), ENT_DEV, 0)
        table = jnp.concatenate([low_rows, high_rows], axis=0)
        edge_pair = jnp.stack([lax.dynamic_slice_in_dim(edge_round, (lower * EDGES_DEV).astype(jnp.int32), EDGES_DEV, 1), lax.dynamic_slice_in_dim(edge_round, (upper * EDGES_DEV).astype(jnp.int32), EDGES_DEV, 1)])
        negative_pair = jnp.stack([lax.dynamic_slice_in_dim(negative_round, (lower * BLOCKS).astype(jnp.int32), BLOCKS, 0), lax.dynamic_slice_in_dim(negative_round, (upper * BLOCKS).astype(jnp.int32), BLOCKS, 0)])
        count_pair = jnp.stack([lax.dynamic_index_in_dim(count_round, lower, 0, keepdims=False), lax.dynamic_index_in_dim(count_round, upper, 0, keepdims=False)]).astype(jnp.int32)
        block_pair = (count_pair + BLOCK - 1) // BLOCK
        grads = jnp.zeros((2 * ENT_DEV, DIM), jnp.float32)
        grads, grad_relation = bucket_pass((grads, grad_relation), table, relations, edge_pair, negative_pair, count_pair, source_shift, target_shift, BLOCK, jnp.int32(0), (block_pair[0] + block_pair[1]).astype(jnp.int32))
        for side, which in ((lower, 0), (upper, 1)):
            offset = (side * ENT_DEV).astype(jnp.int32)
            rows = table[which * ENT_DEV:(which + 1) * ENT_DEV]
            state = lax.dynamic_slice_in_dim(entity_state, offset, ENT_DEV, 0)
            rows, state = adagrad(rows, state, grads[which * ENT_DEV:(which + 1) * ENT_DEV])
            new_entities = lax.dynamic_update_slice_in_dim(new_entities, rows, offset, 0)
            new_state = lax.dynamic_update_slice_in_dim(new_state, state, offset, 0)
        return (new_entities, new_state, grad_relation)
    start = (entities, entity_state, jnp.zeros((REL, DIM), jnp.float32))
    new_entities, new_state, grad_relation = lax.fori_loop(jnp.int32(0), jnp.int32(PARTITIONS // 2), visit_pair, start)
    return (new_entities, new_state, grad_relation)

def reference(entities, entity_state, relations, relation_state, edges, negatives, counts):
    levels = PARTITIONS.bit_length() - 1
    for round_index, bit in enumerate((levels - 1, 0)):
        entities, entity_state, grad_relation = round_pass(entities, entity_state, relations, edges[round_index], negatives[round_index], counts[round_index], 2 ** bit)
        relations, relation_state = adagrad(relations, relation_state, grad_relation)
    return (entities, entity_state, relations, relation_state)
```

```python
import jax
import jax.numpy as jnp
from jax import lax
from jax.sharding import PartitionSpec as P

RATE = 0.2
HIGH = lax.Precision.HIGH
F32 = jnp.float32


def swapped(block, axis, apart):
    count = lax.axis_size(axis)
    route = []
    for low in range(count):
        high = low | 1 << apart
        if high != low and high < count:
            route += [(low, high), (high, low)]
    return lax.ppermute(block, axis, route)


def dot(a, b, ca, cb):
    return lax.dot_general(
        a, b, (((ca,), (cb,)), ((), ())), precision=HIGH, preferred_element_type=F32
    )


def adagrad(param, state, grad):
    new_state = state + jnp.mean(grad * grad, axis=1)
    return (param - RATE * grad / jnp.sqrt(new_state)[:, None], new_state)


def body(entities, entity_state, relations, relation_state, edges, negatives, counts):
    rows, dim = entities.shape
    half = dim // 2
    blocks, neg = negatives.shape[1:]
    slots = edges.shape[2]
    block = slots // blocks
    lane = 128
    levels = lax.axis_size("dom").bit_length() - 1
    bits = (levels - 1, 0)
    infos = []
    for r, bit in enumerate(bits):
        packed = jnp.concatenate([edges[r, 2], negatives[r].reshape(-1), counts[r]])
        infos.append(swapped(packed, "dom", bit))
    for r, bit in enumerate(bits):
        src_hot = (edges[r, 0][:, None] == jnp.arange(rows)[None, :]).astype(F32)
        rel_hot = (edges[r, 1][:, None] == jnp.arange(relations.shape[0])[None, :]).astype(F32)
        s = dot(src_hot, entities, 1, 0)
        w = dot(rel_hot, relations, 1, 0)
        s_re, s_im, w_re, w_im = s[:, :half], s[:, half:], w[:, :half], w[:, half:]
        q = jnp.concatenate([s_re * w_re - s_im * w_im, s_re * w_im + s_im * w_re], axis=1)
        q_in = swapped(q, "dom", bit)
        tgt = infos[r][:slots]
        ids = infos[r][slots : slots + blocks * neg].reshape(blocks, neg)
        live = jnp.arange(slots) < infos[r][slots + blocks * neg]
        hi_hot = (ids[:, :, None] // lane == jnp.arange(rows // lane)).astype(jnp.bfloat16)
        lo_hot = (ids[:, :, None] % lane == jnp.arange(lane)).astype(jnp.bfloat16)
        times = lax.dot_general(
            hi_hot, lo_hot, (((1,), (1,)), ((0,), (0,))), preferred_element_type=F32
        ).reshape(blocks, 1, rows) * (1.0 / neg)
        score = dot(q_in, entities, 1, 1)
        small = jnp.exp(-jnp.abs(score))
        large = 1.0 / (1.0 + small)
        small = small * large
        up_sig = jnp.where(score >= 0, large, small)
        down_sig = jnp.where(score >= 0, small, large)
        weight = (up_sig.reshape(blocks, block, rows) * times).reshape(slots, rows)
        weight -= jnp.where(tgt[:, None] == jnp.arange(rows)[None, :], down_sig, 0.0)
        weight = jnp.where(live[:, None], weight, 0.0)
        u = swapped(dot(weight, entities, 1, 0), "dom", bit)
        grad = dot(weight, q_in, 0, 0)
        u_re, u_im = u[:, :half], u[:, half:]
        s_grad = jnp.concatenate([u_re * w_re + u_im * w_im, u_im * w_re - u_re * w_im], axis=1)
        w_grad = jnp.concatenate([u_re * s_re + u_im * s_im, u_im * s_re - u_re * s_im], axis=1)
        h = lax.psum(dot(rel_hot, w_grad, 0, 0), "dom")
        grad += dot(src_hot, s_grad, 0, 0)
        entities, entity_state = adagrad(entities, entity_state, grad)
        relations, relation_state = adagrad(relations, relation_state, h)
    return (entities, entity_state, relations, relation_state)


def solution(mesh):
    return jax.shard_map(
        body,
        mesh=mesh,
        in_specs=(
            P("dom", None),
            P("dom"),
            P(),
            P(),
            P(None, None, "dom"),
            P(None, "dom", None),
            P(None, "dom"),
        ),
        out_specs=(P("dom", None), P("dom"), P(), P()),
        check_vma=False,
    )
```

```python
import functools

import jax
import jax.numpy as jnp
from jax import lax
from jax.experimental import pallas as pl
from jax.experimental.pallas import tpu as pltpu
from jax.sharding import PartitionSpec as P

RATE = 0.2
HIGH = lax.Precision.HIGH
F32 = jnp.float32


def swapped(block, axis, apart):
    count = lax.axis_size(axis)
    route = []
    for low in range(count):
        high = low | 1 << apart
        if high != low and high < count:
            route += [(low, high), (high, low)]
    return lax.ppermute(block, axis, route)


def dot(a, b, ca, cb):
    return lax.dot_general(
        a, b, (((ca,), (cb,)), ((), ())), precision=HIGH, preferred_element_type=F32
    )


def adagrad(param, state, grad):
    new_state = state + jnp.mean(grad * grad, axis=1)
    return (param - RATE * grad / jnp.sqrt(new_state)[:, None], new_state)


def relation_kernel(levels, dim, table_ref, grad_ref, out_ref, acc, landed, send_sem, recv_sem):
    me = lax.axis_index("dom")
    rows = grad_ref.shape[0]
    core = me % 2

    def side_of(bit):
        return me // 2**bit % 2

    first = list(range(levels))
    second = list(range(levels))
    for low in range(1, levels - 1, 2):
        second[low], second[low + 1] = second[low + 1], second[low]
    sides, peers = [], []
    for a, b in zip(first, second):
        sides.append((1 - core) * side_of(a) + core * side_of(b))
        step_a = (1 - 2 * side_of(a)) * 2**a
        step_b = (1 - 2 * side_of(b)) * 2**b
        peers.append(me + (1 - core) * step_a + core * step_b)

    barrier = pltpu.get_barrier_semaphore()
    for peer in peers:
        pl.semaphore_signal(
            barrier, inc=1, device_id=(peer,), device_id_type=pl.DeviceIdType.MESH
        )
    pl.semaphore_wait(barrier, levels)

    def piece(start, size):
        return pl.ds(pl.multiple_of(start, 8), size)

    start, size, slot = 0, rows, 0
    source = grad_ref
    for step in range(levels):
        size //= 2
        keep = start + sides[step] * size
        give = start + (1 - sides[step]) * size
        copy = pltpu.make_async_remote_copy(
            src_ref=source.at[piece(give, size)],
            dst_ref=landed.at[pl.ds(slot, size)],
            send_sem=send_sem.at[step],
            recv_sem=recv_sem.at[step],
            device_id=(peers[step],),
            device_id_type=pl.DeviceIdType.MESH,
        )
        copy.start()
        copy.wait()
        if step + 1 < levels:
            half = size // 2
            for flip in (1 - sides[step + 1], sides[step + 1]):
                acc[piece(keep + flip * half, half), :] = (
                    source[piece(keep + flip * half, half), :]
                    + landed[piece(slot + flip * half, half), :]
                )
        else:
            acc[piece(keep, size), :] = (
                source[piece(keep, size), :] + landed[pl.ds(slot, size), :]
            )
        source = acc
        start = keep
        slot += size

    grad = acc[piece(start, size), :]
    old = table_ref[piece(start, size), :]
    state = old[:, dim : dim + 1] + jnp.sum(grad * grad, axis=1, keepdims=True) * (1.0 / dim)
    new = old - RATE * grad / jnp.sqrt(state)
    column = lax.broadcasted_iota(jnp.int32, new.shape, 1)
    out_ref[piece(start, size), :] = jnp.where(column == dim, state, new)

    for step in reversed(range(levels)):
        copy = pltpu.make_async_remote_copy(
            src_ref=out_ref.at[piece(start, size)],
            dst_ref=out_ref.at[piece(start, size)],
            send_sem=send_sem.at[levels + step],
            recv_sem=recv_sem.at[levels + step],
            device_id=(peers[step],),
            device_id_type=pl.DeviceIdType.MESH,
        )
        copy.start()
        copy.wait()
        start = start - sides[step] * size
        size *= 2


def relation_update(table, grad, levels, dim, number):
    vmem = pl.BlockSpec(memory_space=pltpu.VMEM)
    return pl.pallas_call(
        functools.partial(relation_kernel, levels, dim),
        out_shape=jax.ShapeDtypeStruct(table.shape, F32),
        in_specs=[vmem, vmem],
        out_specs=vmem,
        scratch_shapes=[
            pltpu.VMEM(table.shape, F32),
            pltpu.VMEM(table.shape, F32),
            pltpu.SemaphoreType.DMA((2 * levels,)),
            pltpu.SemaphoreType.DMA((2 * levels,)),
        ],
        compiler_params=pltpu.CompilerParams(
            collective_id=number, has_side_effects=True, vmem_limit_bytes=32 * 2**20
        ),
    )(table, grad)


def body(entities, entity_state, relations, relation_state, edges, negatives, counts):
    rows, dim = entities.shape
    half = dim // 2
    blocks, neg = negatives.shape[1:]
    slots = edges.shape[2]
    block = slots // blocks
    lane = 128
    levels = lax.axis_size("dom").bit_length() - 1
    bits = (levels - 1, 0)
    rel_rows = relations.shape[0]
    unit = 8 * lax.axis_size("dom")
    wide = -(-(dim + 1) // lane) * lane
    more = -rel_rows % unit
    table = jnp.concatenate(
        [
            jnp.pad(relations, ((0, more), (0, 0))),
            jnp.pad(relation_state, (0, more), constant_values=1.0)[:, None],
            jnp.zeros((rel_rows + more, wide - dim - 1), F32),
        ],
        axis=1,
    )
    infos = []
    for r, bit in enumerate(bits):
        packed = jnp.concatenate([edges[r, 2], negatives[r].reshape(-1), counts[r]])
        infos.append(swapped(packed, "dom", bit))
    for r, bit in enumerate(bits):
        src_hot = (edges[r, 0][:, None] == jnp.arange(rows)[None, :]).astype(F32)
        rel_hot = (edges[r, 1][:, None] == jnp.arange(table.shape[0])[None, :]).astype(F32)
        s = dot(src_hot, entities, 1, 0)
        w = dot(rel_hot, table, 1, 0)[:, :dim]
        s_re, s_im, w_re, w_im = s[:, :half], s[:, half:], w[:, :half], w[:, half:]
        q = jnp.concatenate([s_re * w_re - s_im * w_im, s_re * w_im + s_im * w_re], axis=1)
        q_in = swapped(q, "dom", bit)
        tgt = infos[r][:slots]
        ids = infos[r][slots : slots + blocks * neg].reshape(blocks, neg)
        live = jnp.arange(slots) < infos[r][slots + blocks * neg]
        hi_hot = (ids[:, :, None] // lane == jnp.arange(rows // lane)).astype(jnp.bfloat16)
        lo_hot = (ids[:, :, None] % lane == jnp.arange(lane)).astype(jnp.bfloat16)
        times = lax.dot_general(
            hi_hot, lo_hot, (((1,), (1,)), ((0,), (0,))), preferred_element_type=F32
        ).reshape(blocks, 1, rows) * (1.0 / neg)
        score = dot(q_in, entities, 1, 1)
        small = jnp.exp(-jnp.abs(score))
        large = 1.0 / (1.0 + small)
        small = small * large
        up_sig = jnp.where(score >= 0, large, small)
        down_sig = jnp.where(score >= 0, small, large)
        weight = (up_sig.reshape(blocks, block, rows) * times).reshape(slots, rows)
        weight -= jnp.where(tgt[:, None] == jnp.arange(rows)[None, :], down_sig, 0.0)
        weight = jnp.where(live[:, None], weight, 0.0)
        u = swapped(dot(weight, entities, 1, 0), "dom", bit)
        grad = dot(weight, q_in, 0, 0)
        u_re, u_im = u[:, :half], u[:, half:]
        s_grad = jnp.concatenate([u_re * w_re + u_im * w_im, u_im * w_re - u_re * w_im], axis=1)
        w_grad = jnp.concatenate([u_re * s_re + u_im * s_im, u_im * s_re - u_re * s_im], axis=1)
        w_grad = jnp.pad(w_grad, ((0, 0), (0, wide - dim)))
        table = relation_update(table, dot(rel_hot, w_grad, 0, 0), levels, dim, r)
        grad += dot(src_hot, s_grad, 0, 0)
        entities, entity_state = adagrad(entities, entity_state, grad)
    return (entities, entity_state, table[:rel_rows, :dim], table[:rel_rows, dim])


def solution(mesh):
    return jax.shard_map(
        body,
        mesh=mesh,
        in_specs=(
            P("dom", None),
            P("dom"),
            P(),
            P(),
            P(None, None, "dom"),
            P(None, "dom", None),
            P(None, "dom"),
        ),
        out_specs=(P("dom", None), P("dom"), P(), P()),
        check_vma=False,
    )
```

```python
import functools

import jax
import jax.numpy as jnp
from jax import lax
from jax.experimental import pallas as pl
from jax.experimental.pallas import tpu as pltpu
from jax.sharding import PartitionSpec as P

RATE = 0.2
HIGH = lax.Precision.HIGH
F32 = jnp.float32


def swapped(block, axis, apart):
    count = lax.axis_size(axis)
    route = []
    for low in range(count):
        high = low | 1 << apart
        if high != low and high < count:
            route += [(low, high), (high, low)]
    return lax.ppermute(block, axis, route)


def dot(a, b, ca, cb):
    return lax.dot_general(
        a, b, (((ca,), (cb,)), ((), ())), precision=HIGH, preferred_element_type=F32
    )


def adagrad(param, state, grad):
    new_state = state + jnp.mean(grad * grad, axis=1)
    return (param - RATE * grad / jnp.sqrt(new_state)[:, None], new_state)


def relation_kernel(levels, dim, table_ref, grad_ref, out_ref, acc, landed, send_sem, recv_sem):
    me = lax.axis_index("dom")
    rows = grad_ref.shape[0]
    streams = 3 if rows % (24 * 2**levels) == 0 else 1
    sides = [me // 2**bit % 2 for bit in range(levels)]
    peers = [me + (1 - 2 * sides[bit]) * 2**bit for bit in range(levels)]
    inner = list(range(1, levels - 1))
    orders = []
    for stream in range(streams):
        turn = stream % max(len(inner), 1)
        orders.append([0] + inner[turn:] + inner[:turn] + [levels - 1])

    barrier = pltpu.get_barrier_semaphore()
    for peer in peers:
        pl.semaphore_signal(
            barrier, inc=1, device_id=(peer,), device_id_type=pl.DeviceIdType.MESH
        )
    pl.semaphore_wait(barrier, levels)

    def piece(start, size):
        return pl.ds(pl.multiple_of(start, 8), size)

    def send(source, target, stream, step, phase, bit):
        number = (phase * streams + stream) * levels + step
        copy = pltpu.make_async_remote_copy(
            src_ref=source,
            dst_ref=target,
            send_sem=send_sem.at[number],
            recv_sem=recv_sem.at[number],
            device_id=(peers[bit],),
            device_id_type=pl.DeviceIdType.MESH,
        )
        copy.start()
        return copy

    size = rows // streams
    starts = [stream * size for stream in range(streams)]
    slots = [stream * size for stream in range(streams)]
    source = grad_ref
    for step in range(levels):
        size //= 2
        copies = []
        for stream in range(streams):
            side = sides[orders[stream][step]]
            give = starts[stream] + (1 - side) * size
            copies.append(
                send(
                    source.at[piece(give, size)],
                    landed.at[pl.ds(slots[stream], size)],
                    stream,
                    step,
                    0,
                    orders[stream][step],
                )
            )
        for stream in range(streams):
            keep = starts[stream] + sides[orders[stream][step]] * size
            copies[stream].wait()
            acc[piece(keep, size), :] = (
                source[piece(keep, size), :] + landed[pl.ds(slots[stream], size), :]
            )
            starts[stream] = keep
            slots[stream] += size
        source = acc

    for stream in range(streams):
        own = piece(starts[stream], size)
        grad = acc[own, :]
        old = table_ref[own, :]
        state = old[:, dim : dim + 1] + jnp.sum(grad * grad, axis=1, keepdims=True) * (1.0 / dim)
        new = old - RATE * grad / jnp.sqrt(state)
        column = lax.broadcasted_iota(jnp.int32, new.shape, 1)
        out_ref[own, :] = jnp.where(column == dim, state, new)

    for step in reversed(range(levels)):
        copies = []
        for stream in range(streams):
            own = piece(starts[stream], size)
            copies.append(
                send(out_ref.at[own], out_ref.at[own], stream, step, 1, orders[stream][step])
            )
        for stream in range(streams):
            copies[stream].wait()
            starts[stream] = starts[stream] - sides[orders[stream][step]] * size
        size *= 2


def relation_update(table, grad, levels, dim, number):
    vmem = pl.BlockSpec(memory_space=pltpu.VMEM)
    return pl.pallas_call(
        functools.partial(relation_kernel, levels, dim),
        out_shape=jax.ShapeDtypeStruct(table.shape, F32),
        in_specs=[vmem, vmem],
        out_specs=vmem,
        scratch_shapes=[
            pltpu.VMEM(table.shape, F32),
            pltpu.VMEM(table.shape, F32),
            pltpu.SemaphoreType.DMA((6 * levels,)),
            pltpu.SemaphoreType.DMA((6 * levels,)),
        ],
        compiler_params=pltpu.CompilerParams(
            collective_id=number, has_side_effects=True, vmem_limit_bytes=32 * 2**20
        ),
    )(table, grad)


def body(entities, entity_state, relations, relation_state, edges, negatives, counts):
    rows, dim = entities.shape
    half = dim // 2
    blocks, neg = negatives.shape[1:]
    slots = edges.shape[2]
    block = slots // blocks
    lane = 128
    levels = lax.axis_size("dom").bit_length() - 1
    bits = (levels - 1, 0)
    rel_rows = relations.shape[0]
    unit = 8 * lax.axis_size("dom")
    wide = -(-(dim + 1) // lane) * lane
    more = -rel_rows % unit
    table = jnp.concatenate(
        [
            jnp.pad(relations, ((0, more), (0, 0))),
            jnp.pad(relation_state, (0, more), constant_values=1.0)[:, None],
            jnp.zeros((rel_rows + more, wide - dim - 1), F32),
        ],
        axis=1,
    )
    infos = []
    for r, bit in enumerate(bits):
        packed = jnp.concatenate([edges[r, 2], negatives[r].reshape(-1), counts[r]])
        infos.append(swapped(packed, "dom", bit))
    for r, bit in enumerate(bits):
        src_hot = (edges[r, 0][:, None] == jnp.arange(rows)[None, :]).astype(F32)
        rel_hot = (edges[r, 1][:, None] == jnp.arange(table.shape[0])[None, :]).astype(F32)
        s = dot(entities, src_hot, 0, 1)
        w = dot(table, rel_hot, 0, 1)[:dim]
        s_re, s_im, w_re, w_im = s[:half], s[half:], w[:half], w[half:]
        q = jnp.concatenate([s_re * w_re - s_im * w_im, s_re * w_im + s_im * w_re], axis=0)
        q_in = swapped(q, "dom", bit)
        tgt = infos[r][:slots]
        ids = infos[r][slots : slots + blocks * neg].reshape(blocks, neg)
        live = jnp.arange(slots) < infos[r][slots + blocks * neg]
        hi_hot = (ids[:, :, None] // lane == jnp.arange(rows // lane)).astype(jnp.bfloat16)
        lo_hot = (ids[:, :, None] % lane == jnp.arange(lane)).astype(jnp.bfloat16)
        times = lax.dot_general(
            hi_hot, lo_hot, (((1,), (1,)), ((0,), (0,))), preferred_element_type=F32
        ).reshape(blocks, 1, rows) * (1.0 / neg)
        score = dot(q_in, entities, 0, 1)
        small = jnp.exp(-jnp.abs(score))
        large = 1.0 / (1.0 + small)
        small = small * large
        up_sig = jnp.where(score >= 0, large, small)
        down_sig = jnp.where(score >= 0, small, large)
        weight = (up_sig.reshape(blocks, block, rows) * times).reshape(slots, rows)
        weight -= jnp.where(tgt[:, None] == jnp.arange(rows)[None, :], down_sig, 0.0)
        weight = jnp.where(live[:, None], weight, 0.0)
        u = swapped(dot(entities, weight, 0, 1), "dom", bit)
        grad = dot(weight, q_in, 0, 1)
        u_re, u_im = u[:half], u[half:]
        s_grad = jnp.concatenate([u_re * w_re + u_im * w_im, u_im * w_re - u_re * w_im], axis=0)
        w_grad = jnp.concatenate([u_re * s_re + u_im * s_im, u_im * s_re - u_re * s_im], axis=0)
        w_grad = jnp.pad(w_grad, ((0, wide - dim), (0, 0)))
        table = relation_update(table, dot(rel_hot, w_grad, 0, 1), levels, dim, r)
        grad += dot(src_hot, s_grad, 0, 1)
        entities, entity_state = adagrad(entities, entity_state, grad)
    return (entities, entity_state, table[:rel_rows, :dim], table[:rel_rows, dim])


def solution(mesh):
    return jax.shard_map(
        body,
        mesh=mesh,
        in_specs=(
            P("dom", None),
            P("dom"),
            P(),
            P(),
            P(None, None, "dom"),
            P(None, "dom", None),
            P(None, "dom"),
        ),
        out_specs=(P("dom", None), P("dom"), P(), P()),
        check_vma=False,
    )
```
